32 devices in a mesh: tx: 4 (over x, core), py: 2 (over y), pz: 4 (over z).
Axes of the slice: x: 2, y: 2, z: 4, core: 2. Of those that a mesh axis runs over, the one named last changes fastest.
Arguments:
- fields: float32 [16, 2, 128, 128, 128], P('tx', None, 'py', 'pz'), may hold values from 0.5 to 1.5
- sources: float32 [16, 2, 128, 128, 128], P('tx', None, 'py', 'pz'), may hold values from -12 to 12
- green: float32 [2, 128, 128, 128], P(None, 'pz', 'py'), may hold values from -6 to 6
Outputs:
- contrast_fine: float32 [2, 256, 256, 256], P(None, 'py', 'pz')
- scattered: float32 [4, 2, 256, 256, 256], P('tx', None, 'py', 'pz')
The draws below stay inside these ranges and needn't reach their ends.
All inputs are finite; a program needn't handle non-finite values.
Results may differ from the reference program's by a relative error of at most 0.00014.
Values sent between devices are 32-bit elements; how exact they have to be, the bound alone decides.
A program may use at most 192 MiB of HBM per device.

```python
import jax
import jax.numpy as jnp
from jax import lax

COARSE = 128
FINE = 256
PART_DEV = 4
TRANSMITTERS = 16


def levels(key, dims, pieces, least, largest):
    def one(axis_at, blocks):
        steps = jax.random.uniform(jax.random.fold_in(jax.random.fold_in(key, 6), axis_at), (blocks,), jnp.float32, least / len(pieces), largest / len(pieces))
        return jnp.repeat(jnp.exp(steps), dims[axis_at] // blocks).reshape((-1,) + (1,) * (len(dims) - axis_at - 1))

    level = one(*pieces[0])
    for cut in pieces[1:]:
        level = level * one(*cut)
    return level


def bell_draw(key, dims, deviation, limit, split=(), held_as=jnp.bfloat16):
    level = levels(key, dims, split, -0.22, 0.18) if split else 1.0
    array = jax.random.normal(key, dims, jnp.float32) * deviation * level
    return jnp.minimum(jnp.maximum(array, -limit), limit).astype(held_as)


def setup_inputs(seed: int = 0) -> dict:
    arg_keys = jax.random.split(jax.random.key(seed), 4)
    return {
        "fields": jnp.clip(0.5 + 1.0 * jax.random.uniform(arg_keys[0], (TRANSMITTERS, 2, COARSE, COARSE, COARSE), jnp.float32) ** levels(arg_keys[0], (TRANSMITTERS, 2, COARSE, COARSE, COARSE), ((0, 4), (2, 2), (3, 4)), -0.2, 0.2), 0.5, 1.5),
        "sources": bell_draw(arg_keys[1], (TRANSMITTERS, 2, COARSE, COARSE, COARSE), 2.0, 12.0, ((0, 4), (2, 2), (3, 4)), jnp.float32),
        "green": bell_draw(arg_keys[2], (2, COARSE, COARSE, COARSE), 1.0, 6.0, ((1, 4), (2, 2)), jnp.float32),
    }


def placed_indices():
    indices = jnp.arange(COARSE, dtype=jnp.int32)
    return jnp.where(indices < COARSE // 2, indices, indices - COARSE + FINE).astype(jnp.int32)


def place_fine(values):
    placed = placed_indices()
    padded = jnp.zeros((FINE, FINE, FINE), values.dtype)
    return padded.at[placed[:, None, None], placed[None, :, None], placed[None, None, :]].set(values)


def prolong(coarse_field):
    spectrum = jnp.fft.fftn(coarse_field)
    return jnp.fft.ifftn(place_fine(spectrum)) * ((FINE / COARSE) ** 3)


def reference(fields, sources, green):
    field_real = fields[:, 0]
    field_imag = fields[:, 1]
    source_real = sources[:, 0]
    source_imag = sources[:, 1]
    numer_real = jnp.sum(source_real * field_real + source_imag * field_imag, axis=0)
    numer_imag = jnp.sum(source_imag * field_real - source_real * field_imag, axis=0)
    denominator = jnp.sum(field_real * field_real + field_imag * field_imag, axis=0)
    contrast = (numer_real / denominator) + 1j * (numer_imag / denominator)
    contrast_fine = prolong(contrast)
    green_spectrum = place_fine(jnp.transpose(green[0] + 1j * green[1], (2, 1, 0)))

    def scatter_one(source_one):
        fine_source = prolong(source_one[0] + 1j * source_one[1])
        domain_field = jnp.fft.ifftn(green_spectrum * jnp.fft.fftn(fine_source))
        product = contrast_fine * domain_field
        return jnp.stack([jnp.real(product), jnp.imag(product)]).astype(jnp.float32)

    scattered = lax.map(scatter_one, sources[::PART_DEV])
    fine_parts = jnp.stack([jnp.real(contrast_fine), jnp.imag(contrast_fine)]).astype(jnp.float32)
    return fine_parts, scattered
```

```python
import functools
import math

import jax
import jax.numpy as jnp
import ml_dtypes
import numpy as np
from jax import lax
from jax.experimental import pallas as pl
from jax.experimental.pallas import tpu as pltpu
from jax.sharding import PartitionSpec as P

F32 = jnp.float32
BF16 = jnp.bfloat16
NN = (((1,), (0,)), ((), ()))
NT = (((1,), (1,)), ((), ()))
MESH = pl.DeviceIdType.MESH
ROWS = 8
GROUPS = 4
PARTS = 4


def signed(count):
    index = np.arange(count)
    return np.where(index < count // 2, index, index - count)


def forward_matrix(coarse):
    index = np.arange(coarse)
    return np.exp(-2j * np.pi * ((index[:, None] * index[None, :]) % coarse) / coarse)


def inverse_matrix(coarse, fine):
    phases = (np.arange(fine)[:, None] * signed(coarse)[None, :]) % fine
    return np.exp(2j * np.pi * phases / fine) / coarse


def block_form(matrix):
    re, im = matrix.real, matrix.imag
    return np.stack([np.stack([re, -im], 1), np.stack([im, re], 1)], 0)


def halves(matrix):
    high = matrix.astype(ml_dtypes.bfloat16)
    low = (matrix - high.astype(np.float64)).astype(ml_dtypes.bfloat16)
    return high, low


def left_table(matrix):
    high, low = halves(matrix)
    return jnp.asarray(np.concatenate([high, high, low], axis=-1))


def right_table(matrix):
    high, low = halves(matrix)
    return jnp.asarray(np.concatenate([high, high, low], axis=-2))


def split(x):
    high = x.astype(BF16)
    return high, (x - high.astype(F32)).astype(BF16)


def product_left(m, x, dims=NN):
    high, low = split(x)
    axis = dims[0][1][0]
    wide = jnp.concatenate([high, low, high], axis=axis)
    return lax.dot_general(m, wide, dimension_numbers=dims, preferred_element_type=F32)


def product_right(x, m):
    high, low = split(x)
    wide = jnp.concatenate([high, low, high], axis=1)
    return lax.dot_general(wide, m, dimension_numbers=NN, preferred_element_type=F32)


def times_i(x):
    half = x.shape[1] // 2
    return jnp.concatenate([-x[:, half:], x[:, :half]], axis=1)


def flip(me, bit):
    return me + bit - 2 * bit * ((me // bit) % 2)


def flips(me, code):
    for bit in (1, 2):
        if code & bit:
            me = flip(me, bit)
    return me


def remote(src, dst, sends, recvs, where):
    return pltpu.make_async_remote_copy(
        src_ref=src, dst_ref=dst, send_sem=sends, recv_sem=recvs,
        device_id=where, device_id_type=MESH,
    )


def exchange_body(
    fields, sources, green, h_s1, h_top, h_f2, h_inv, h_first, h_mid, h_fc,
    ts_out, tc_out,
    xs, s1, yr, s2, zr, gb, s4, fin, fb, sb, sums, cr, xr, cz, cg, st,
    w_s1, w_top, w_f2, w_inv, w_first, w_mid, w_fc,
    load_sem, step_sem, out_sem, local_sem,
    y_s, y_r, z_s, z_r, g_s, g_r, core_s, core_r, x_s, x_r, zc_s, zc_r,
    cy_s, cy_r, cx_s, cx_r, cc_s, cc_r, zb_s, zb_r, yh_s, yh_r,
):
    t, y, z = lax.axis_index("tx"), lax.axis_index("py"), lax.axis_index("pz")
    oy = 1 - y
    z_peer = [flips(z, j) for j in (1, 2, 3)]
    to_z = [{"pz": p} for p in z_peer]
    to_y = {"py": oy}
    core, far = flip(t, 1), flip(t, 2)
    to_core, to_x = {"tx": core}, {"tx": far}
    x_chunks = xs.shape[0]
    k_own = gb.shape[1]
    part = sums.shape[2]
    f_chunks = fin.shape[0]
    rows_h = part // PARTS
    lanes = s1.shape[5]
    coarse = green.shape[3]
    f1 = st.shape[1]

    loads = [
        pltpu.make_async_copy(sources.at[0, :, :, pl.ds(c * ROWS, ROWS), :], xs.at[c], load_sem.at[c])
        for c in range(x_chunks)
    ]
    tables = [
        pltpu.make_async_copy(src, dst, load_sem.at[x_chunks + i])
        for i, (src, dst) in enumerate(
            [
                (h_s1, w_s1), (h_top.at[y], w_top), (h_f2, w_f2), (h_inv, w_inv),
                (h_mid.at[z], w_mid), (h_first.at[y], w_first), (h_fc.at[y], w_fc),
                (green.at[:, pl.ds(y * k_own, k_own)], gb.at[:, :, y]),
            ]
        )
    ]
    order = (1, 3, 0, 2)
    per_block = part // ROWS

    def step_copies(i):
        row = flips(t, order[i // per_block]) * part + (i % per_block) * ROWS
        at = pl.ds(row, ROWS)
        slot = i % 2
        return (
            pltpu.make_async_copy(fields.at[:, :, at], fb.at[slot], step_sem.at[0, slot]),
            pltpu.make_async_copy(sources.at[:, :, at], sb.at[slot], step_sem.at[1, slot]),
        )

    tables[0].start()
    for c in loads:
        c.start()
    tables[1].start()
    for i in range(2):
        for c in step_copies(i):
            c.start()
    for c in tables[2:]:
        c.start()

    barrier = pltpu.get_barrier_semaphore()
    peers = to_z + [to_y, to_core, to_x]
    for where in peers:
        pl.semaphore_signal(barrier, inc=1, device_id=where, device_id_type=MESH)
    pl.semaphore_wait(barrier, len(peers))

    tables[0].wait()
    for c in loads:
        c.wait()

    def depth(c, _):
        for s in range(ROWS):
            re, im = xs[c, 0, :, s, :], xs[c, 1, :, s, :]
            both = jnp.concatenate(
                [jnp.concatenate([re, -im], axis=1), jnp.concatenate([im, re], axis=1)], axis=0
            )
            out = product_left(w_s1[...], both, NT)
            s1[:, :, :, c, s, :] = out.reshape(s1.shape[0], s1.shape[1], s1.shape[2], lanes)
        return 0

    lax.fori_loop(0, x_chunks, depth, 0)

    y_copies = [remote(s1.at[oy, g], yr.at[g], y_s.at[g], y_r.at[g], to_y) for g in range(GROUPS)]
    for c in y_copies:
        c.start()

    core_copies = [
        remote(sums.at[j], cr.at[n], core_s.at[n], core_r.at[n], to_core)
        for n, j in enumerate((1, 3))
    ]
    steps = len(order) * per_block

    def sum_step(i):
        slot, block, base = i % 2, order[i // per_block], (i % per_block) * ROWS
        for c in step_copies(i):
            c.wait()

        def row(r, _):
            total = None
            for k in range(fb.shape[1]):
                fr, fi = fb[slot, k, 0, r], fb[slot, k, 1, r]
                sr, si = sb[slot, k, 0, r], sb[slot, k, 1, r]
                term = (sr * fr + si * fi, si * fr - sr * fi, fr * fr + fi * fi)
                total = term if total is None else tuple(a + b for a, b in zip(total, term))
            for n in range(3):
                sums[block, n, base + r] = total[n]
            return 0

        lax.fori_loop(0, ROWS, row, 0)
        if i + 2 < steps:
            for c in step_copies(i + 2):
                c.start()

    def sum_block(b):
        for i in range(b * per_block, (b + 1) * per_block):
            sum_step(i)

    def z_copy(g, n):
        p = z_peer[n]
        return remote(s2.at[g, p], zr.at[g, :, z], z_s.at[g, n], z_r.at[g, n], to_z[n])

    def top(g):
        y_copies[g].wait_recv()
        rows = s1.shape[2] * s1.shape[3] * ROWS
        own = s1[y, g].reshape(rows, lanes)
        other = yr[g].reshape(rows, lanes)
        out = product_right(jnp.concatenate([own, other], axis=1), w_top[...])
        s2[g] = out.reshape(s2.shape[1:])
        for n in (2, 1, 0):
            z_copy(g, n).start()
        zr[g, :, z] = s2[g, z]

    sum_block(0)
    core_copies[0].start()
    sum_block(1)
    core_copies[1].start()
    tables[1].wait()
    top(0)
    green_copy = remote(
        green.at[:, pl.ds(oy * k_own, k_own)], gb.at[:, :, y], g_s.at[0], g_r.at[0], to_y
    )
    sum_block(2)
    sum_block(3)
    top(1)
    green_copy.start()
    for n, j in enumerate((0, 2)):
        core_copies[n].wait_recv()

        def add(r, _, n=n, j=j):
            for k in range(3):
                sums[j, k, r] = sums[j, k, r] + cr[n, k, r]
            return 0

        lax.fori_loop(0, part, add, 0)
    x_copies = []
    for h in range(PARTS):
        at = pl.ds(h * rows_h, rows_h)
        x_copies.append(remote(sums.at[2, :, at], xr.at[:, at], x_s.at[h], x_r.at[h], to_x))
    for c in x_copies:
        c.start()
    top(2)
    top(3)

    def middle(g):
        for n in range(3):
            z_copy(g, n).wait_recv()

        def one(i, _):
            x = zr[g, i].reshape(coarse, 2 * coarse)
            v = product_left(w_f2[...], jnp.concatenate([x, times_i(x)], axis=0))
            k = g * (k_own // GROUPS) + i
            gr, gi = gb[0, k].reshape(coarse, coarse), gb[1, k].reshape(coarse, coarse)
            vr, vi = v[:, :coarse], v[:, coarse:]
            w = jnp.concatenate([vr * gr - vi * gi, vr * gi + vi * gr], axis=1)
            u = product_left(w_inv[...], jnp.concatenate([w, times_i(w)], axis=0))
            s4[:, :, k] = u.reshape(s4.shape[0], s4.shape[1], ROWS, 2 * coarse)
            return 0

        lax.fori_loop(0, k_own // GROUPS, one, 0)

    def z_slice(h, src):
        return cz.at[:, pl.ds(h * rows_h, rows_h), src]

    def zc_copy(h, kind):
        src = z_peer[1] if kind == 2 else z
        where = to_z[1] if kind == 0 else to_z[0]
        return remote(z_slice(h, src), z_slice(h, src), zc_s.at[kind, h], zc_r.at[kind, h], where)

    def ratio(h):
        x_copies[h].wait_recv()
        for r in range(h * rows_h, (h + 1) * rows_h):
            nr = sums[0, 0, r] + xr[0, r]
            ni = sums[0, 1, r] + xr[1, r]
            d = sums[0, 2, r] + xr[2, r]
            cz[0, r, z] = nr / d
            cz[1, r, z] = ni / d
        zc_copy(h, 0).start()
        zc_copy(h, 1).start()

    tables[2].wait()
    tables[3].wait()
    tables[7].wait()
    green_copy.wait_recv()
    middle(0)
    for h in range(PARTS):
        ratio(h)
    middle(1)
    middle(2)
    for h in range(PARTS):
        zc_copy(h, 0).wait_recv()
        zc_copy(h, 2).start()
    middle(3)

    def zb_copy(j, n):
        return remote(
            s4.at[z_peer[n], j], fin.at[j, y, z], zb_s.at[j, n], zb_r.at[j, n], to_z[n]
        )

    own_copy = pltpu.make_async_copy(s4.at[z], fin.at[:, y, z], local_sem.at[0])
    own_copy.start()

    def send_z(j, _):
        for n in (2, 1, 0):
            zb_copy(j, n).start()
        return 0

    lax.fori_loop(0, f_chunks, send_z, 0)

    def piece(a, b, h):
        return cg.at[a, b, :, :, pl.ds(h * rows_h, rows_h)]

    def pass_on(a, b, h, sends, recvs, where):
        return remote(piece(a, b, h), piece(a, b, h), sends, recvs, where)

    def cy_copy(h):
        return pass_on(y, t, h, cy_s.at[h], cy_r.at[h], to_y)

    def cx_copy(n, h):
        return pass_on((y, oy)[n], t, h, cx_s.at[n, h], cx_r.at[n, h], to_x)

    def cc_copy(n, h):
        return pass_on((y, oy)[n % 2], (t, far)[n // 2], h, cc_s.at[n, h], cc_r.at[n, h], to_core)

    tables[4].wait()
    half = cg.shape[2] * ROWS

    def refine(h):
        zc_copy(h, 1).wait_recv()
        zc_copy(h, 2).wait_recv()
        for r in range(h * rows_h, (h + 1) * rows_h):
            x = jnp.concatenate([cz[0, r].reshape(coarse, coarse), cz[1, r].reshape(coarse, coarse)], axis=0)
            out = product_left(w_mid[...], x)
            for c in range(2):
                cg[y, t, :, c, r] = out[c * half : (c + 1) * half].reshape(cg.shape[2], ROWS, coarse)
        cy_copy(h).start()
        cx_copy(0, h).start()
        cc_copy(0, h).start()

    for h in range(PARTS):
        refine(h)

    def yh_copy(j):
        return remote(fin.at[j, y], fin.at[j, y], yh_s.at[j], yh_r.at[j], to_y)

    def out_copy(target, j, slot):
        return pltpu.make_async_copy(
            st.at[slot], target.at[:, pl.ds(j * ROWS, ROWS), :], out_sem.at[slot]
        )

    def emit(out, slot, s):
        st[slot, :, s, pl.ds(0, coarse)] = out[:f1]
        st[slot, :, s, pl.ds(coarse, coarse)] = out[f1:]

    def first_spec(j, slot):
        for s in range(ROWS):
            x = fin[j, :, :, :, s, :].reshape(coarse, 2 * coarse)
            emit(product_left(w_first[...], x, NT), slot, s)
        out_copy(ts_out, j, slot).start()

    def first_contrast(j, slot):
        for s in range(ROWS):
            x = cg[:, :, j, :, :, s, :].reshape(2 * coarse, coarse)
            emit(product_left(w_fc[...], x), slot, s)
        out_copy(tc_out, j, slot).start()

    own_copy.wait()
    tables[5].wait()
    tables[6].wait()
    lag = 2

    def forward(j, _):
        for n in range(3):
            zb_copy(j, n).wait_recv()
        yh_copy(j).start()

        @pl.when(j == 1)
        def _():
            for h in range(PARTS):
                cy_copy(h).wait_recv()
                cx_copy(1, h).start()
                cc_copy(1, h).start()

        @pl.when(j == 3)
        def _():
            for h in range(PARTS):
                cx_copy(0, h).wait_recv()
                cc_copy(2, h).start()

        @pl.when(j == 5)
        def _():
            for h in range(PARTS):
                cx_copy(1, h).wait_recv()
                cc_copy(3, h).start()

        @pl.when(j >= lag)
        def _():
            yh_copy(j - lag).wait_recv()

            @pl.when(j > lag)
            def _():
                out_copy(ts_out, j - lag - 1, 0).wait()

            first_spec(j - lag, 0)

        return 0

    lax.fori_loop(0, f_chunks, forward, 0)

    for h in range(PARTS):
        for n in range(4):
            cc_copy(n, h).wait_recv()

    def contrast_step(j, _):
        @pl.when(j > 0)
        def _():
            out_copy(tc_out, j - 1, 1).wait()

        first_contrast(j, 1)
        return 0

    lax.fori_loop(0, f_chunks, contrast_step, 0)

    def tail(j, _):
        yh_copy(j).wait_recv()
        out_copy(ts_out, j - 1, 0).wait()
        first_spec(j, 0)
        return 0

    lax.fori_loop(f_chunks - lag, f_chunks, tail, 0)

    for c in y_copies + core_copies + x_copies + [green_copy]:
        c.wait_send()
    for g in range(GROUPS):
        for n in range(3):
            z_copy(g, n).wait_send()
    for h in range(PARTS):
        for n in range(3):
            zc_copy(h, n).wait_send()
        cy_copy(h).wait_send()
        for n in range(2):
            cx_copy(n, h).wait_send()
        for n in range(4):
            cc_copy(n, h).wait_send()

    def drain(j, _):
        for n in range(3):
            zb_copy(j, n).wait_send()
        yh_copy(j).wait_send()
        return 0

    lax.fori_loop(0, f_chunks, drain, 0)
    out_copy(tc_out, f_chunks - 1, 1).wait()
    out_copy(ts_out, f_chunks - 1, 0).wait()


def last_body(m3_ref, m3c_ref, ts_ref, tc_ref, c_ref, o_ref):
    f1, rows, wide = ts_ref.shape
    fine = m3_ref.shape[1] // 2
    step = max(1, 256 // rows)
    for b in range(0, f1, step):
        at = slice(b, b + step)
        d = product_right(ts_ref[at].reshape(step * rows, wide), m3_ref[...])
        c = product_right(tc_ref[at].reshape(step * rows, wide), m3c_ref[...])
        dr, di, cr, ci = d[:, :fine], d[:, fine:], c[:, :fine], c[:, fine:]
        shape = (step, rows, fine)
        c_ref[0, at] = cr.reshape(shape)
        c_ref[1, at] = ci.reshape(shape)
        o_ref[0, 0, at] = (cr * dr - ci * di).reshape(shape)
        o_ref[0, 1, at] = (cr * di + ci * dr).reshape(shape)


def fused_device(tx, py, pz, fields, sources, green):
    coarse = fields.shape[4]
    fine = 2 * coarse
    many = fields.shape[0]
    x1, x2 = fields.shape[2], fields.shape[3]
    f1, f2 = fine // py, fine // pz
    lanes = 2 * x1
    part = x1 // tx
    k3 = coarse // pz
    k_own = k3 // py
    k_group = k_own // GROUPS
    x_chunks, f_chunks = x2 // ROWS, f2 // ROWS

    fwd, inv = forward_matrix(coarse), inverse_matrix(coarse, fine)
    refined = inv @ fwd
    ri = lambda m: np.concatenate([m.real, m.imag], axis=1)
    grid = np.arange(coarse).reshape(pz, py, GROUPS, k_group)
    rows_s1 = grid.transpose(1, 2, 0, 3).reshape(-1)
    rows_k3 = grid.transpose(1, 0, 2, 3).reshape(-1)
    h_s1 = left_table(ri(fwd)[rows_s1])
    top = block_form(fwd).reshape(2 * coarse, 2, py, x1).transpose(2, 1, 3, 0)
    h_top = right_table(
        np.stack([top[[q, 1 - q]].reshape(2 * coarse, 2 * coarse) for q in range(py)])
    )
    h_f2 = left_table(ri(fwd))
    h_inv = left_table(ri(inv))
    first = block_form(inv).reshape(2, py, f1, 2 * coarse).transpose(1, 0, 2, 3)
    h_first = left_table(first.reshape(py, 2 * f1, 2 * coarse))
    mid = block_form(refined).reshape(2, pz, f2, 2 * coarse).transpose(1, 0, 2, 3)
    h_mid = left_table(mid.reshape(pz, 2 * f2, 2 * coarse))
    fc = block_form(refined).reshape(2, py, f1, 2, py, tx, part).transpose(1, 0, 2, 4, 5, 3, 6)
    h_fc = left_table(fc.reshape(py, 2 * f1, 2 * coarse))
    last = block_form(inv).transpose(2, 3, 0, 1)[:, rows_k3].reshape(2 * coarse, 2 * fine)
    last_c = block_form(refined).transpose(2, 3, 0, 1).reshape(2 * coarse, 2 * fine)
    m3, m3c = right_table(last), right_table(last_c)

    vm = lambda *dims: pltpu.VMEM(dims, F32)
    wm = lambda *dims: pltpu.VMEM(dims, BF16)
    dma = lambda *dims: pltpu.SemaphoreType.DMA(dims)
    pair = lambda *dims: [dma(*dims), dma(*dims)]
    wide = 2 * coarse
    scratch = [
        vm(x_chunks, 2, x1, ROWS, coarse),
        vm(py, GROUPS, pz * k_group, x_chunks, ROWS, lanes),
        vm(GROUPS, pz * k_group, x_chunks, ROWS, lanes),
        vm(GROUPS, pz, k_group, x2, wide),
        vm(GROUPS, k_group, pz, x2, wide),
        vm(2, k_own, py, coarse // py, coarse),
        vm(pz, f_chunks, k_own, ROWS, wide),
        vm(f_chunks, py, pz, k_own, ROWS, wide),
        vm(2, many, 2, ROWS, x2, coarse),
        vm(2, many, 2, ROWS, x2, coarse),
        vm(tx, 3, part, x2, coarse),
        vm(2, 3, part, x2, coarse),
        vm(3, part, x2, coarse),
        vm(2, part, pz, x2, coarse),
        vm(py, tx, f_chunks, 2, part, ROWS, coarse),
        vm(2, f1, ROWS, wide),
        wm(*h_s1.shape), wm(*h_top.shape[1:]), wm(*h_f2.shape), wm(*h_inv.shape),
        wm(*h_first.shape[1:]), wm(*h_mid.shape[1:]), wm(*h_fc.shape[1:]),
        dma(x_chunks + 8), dma(2, 2), dma(2), dma(1),
        *pair(GROUPS), *pair(GROUPS, 3), *pair(1), *pair(2), *pair(PARTS), *pair(3, PARTS),
        *pair(PARTS), *pair(2, PARTS), *pair(4, PARTS), *pair(f_chunks, 3), *pair(f_chunks),
    ]
    middle_shape = jax.ShapeDtypeStruct((f1, f2, wide), F32)
    operands = (fields, sources, green, h_s1, h_top, h_f2, h_inv, h_first, h_mid, h_fc)
    anywhere = pl.BlockSpec(memory_space=pl.ANY)
    ts, tc = pl.pallas_call(
        exchange_body,
        in_specs=[anywhere] * len(operands),
        out_specs=[anywhere] * 2,
        out_shape=[middle_shape] * 2,
        scratch_shapes=scratch,
        name="exchange",
        compiler_params=pltpu.CompilerParams(
            collective_id=0, has_side_effects=True, vmem_limit_bytes=63 * 2**20
        ),
    )(*operands)

    blocked = pl.BlockSpec((f1, ROWS, wide), lambda i: (0, i, 0))
    whole = pl.BlockSpec(m3.shape, lambda i: (0, 0))
    return pl.pallas_call(
        last_body,
        grid=(f_chunks,),
        in_specs=[whole, whole, blocked, blocked],
        out_specs=[
            pl.BlockSpec((2, f1, ROWS, fine), lambda i: (0, 0, i, 0)),
            pl.BlockSpec((1, 2, f1, ROWS, fine), lambda i: (0, 0, 0, i, 0)),
        ],
        out_shape=[
            jax.ShapeDtypeStruct((2, f1, f2, fine), F32),
            jax.ShapeDtypeStruct((1, 2, f1, f2, fine), F32),
        ],
        name="last",
        compiler_params=pltpu.CompilerParams(vmem_limit_bytes=48 * 2**20),
    )(m3, m3c, ts, tc)


def fourier_matrix(out_index, in_index, period, exponent_sign, weight):
    phases = out_index[:, None] * in_index[None, :] % period
    angles = exponent_sign * 2.0 * math.pi / period * phases.astype(jnp.float32)
    cosine = weight * jnp.cos(angles)
    sine_part = weight * jnp.sin(angles)
    return jnp.stack([jnp.stack([cosine, -sine_part], 1), jnp.stack([sine_part, cosine], 1)], 0)


def local_step(values, matrix):
    return jnp.einsum("fcxyl,dkcl->fdyxk", values, matrix, precision=lax.Precision.HIGHEST)


def remote_step(values, matrix):
    return jnp.einsum("fclxy,dkcl->fdxyk", values, matrix, precision=lax.Precision.HIGHEST)


def turn(values, matrix, axis):
    return remote_step(lax.all_to_all(values, axis, split_axis=4, concat_axis=2, tiled=True), matrix)


def forward_pass(values, matrix):
    return turn(turn(local_step(values, matrix), matrix, "pz"), matrix, "py")


def inverse_pass(values, matrix):
    return turn(turn(local_step(values, matrix), matrix, "py"), matrix, "pz")


def complex_product(first_factor, second_factor):
    real_part = first_factor[0] * second_factor[0] - first_factor[1] * second_factor[1]
    imag_part = first_factor[0] * second_factor[1] + first_factor[1] * second_factor[0]
    return jnp.stack([real_part, imag_part])


def general_device(fields, sources, green):
    coarse = fields.shape[4]
    fine = 2 * coarse
    index = jnp.arange(coarse, dtype=jnp.int32)
    fine_index = jnp.arange(fine, dtype=jnp.int32)
    signed_coarse = jnp.where(index < coarse // 2, index, index - coarse)
    unit_coarse = jnp.ones((coarse, 1), F32)
    unit_fine = jnp.ones((fine, 1), F32)
    coarse_forward = fourier_matrix(index, index, coarse, -1.0, unit_coarse)
    padded_inverse = fourier_matrix(fine_index, signed_coarse, fine, 1.0, unit_fine / coarse)
    fr, fi, sr, si = fields[:, 0], fields[:, 1], sources[:, 0], sources[:, 1]
    numer_re = jnp.sum(sr * fr + si * fi, axis=0)
    numer_im = jnp.sum(si * fr - sr * fi, axis=0)
    denom = jnp.sum(fr * fr + fi * fi, axis=0)
    numer_re, numer_im, denom = lax.psum((numer_re, numer_im, denom), "tx")
    contrast = jnp.stack([numer_re / denom, numer_im / denom])[None]
    contrast_fine = inverse_pass(forward_pass(contrast, coarse_forward), padded_inverse)[0]
    spectrum = forward_pass(sources[0:1], coarse_forward)
    weighted = complex_product(spectrum[0], green)[None]
    domain_field = inverse_pass(weighted, padded_inverse)[0]
    return contrast_fine, complex_product(contrast_fine, domain_field)[None]


def solution(mesh):
    tx, py, pz = mesh.shape["tx"], mesh.shape["py"], mesh.shape["pz"]

    def on_device(fields, sources, green):
        x1, x2, coarse = fields.shape[2:]
        fused = (
            tx == 4 and py == 2 and pz == 4
            and coarse % 128 == 0 and (2 * x1) % 128 == 0 and x1 % (tx * ROWS) == 0
            and x2 % ROWS == 0 and (2 * coarse // pz) % ROWS == 0
            and coarse % (pz * py * GROUPS) == 0 and x1 % (tx * PARTS) == 0
            and coarse * coarse * coarse <= 2**21
        )
        if fused:
            return fused_device(tx, py, pz, fields, sources, green)
        return general_device(fields, sources, green)

    placed = (
        P("tx", None, "py", "pz", None),
        P("tx", None, "py", "pz", None),
        P(None, "pz", "py", None),
    )
    return jax.shard_map(
        on_device,
        mesh=mesh,
        in_specs=placed,
        out_specs=(P(None, "py", "pz", None), P("tx", None, "py", "pz", None)),
        check_vma=False,
    )
```

```python
import functools
import math

import jax
import jax.numpy as jnp
import ml_dtypes
import numpy as np
from jax import lax
from jax.experimental import pallas as pl
from jax.experimental.pallas import tpu as pltpu
from jax.sharding import PartitionSpec as P

F32 = jnp.float32
BF16 = jnp.bfloat16
NN = (((1,), (0,)), ((), ()))
NT = (((1,), (1,)), ((), ()))
MESH = pl.DeviceIdType.MESH
ROWS = 8
GROUPS = 4
PARTS = 4


def signed(count):
    index = np.arange(count)
    return np.where(index < count // 2, index, index - count)


def forward_matrix(coarse):
    index = np.arange(coarse)
    return np.exp(-2j * np.pi * ((index[:, None] * index[None, :]) % coarse) / coarse)


def inverse_matrix(coarse, fine):
    phases = (np.arange(fine)[:, None] * signed(coarse)[None, :]) % fine
    return np.exp(2j * np.pi * phases / fine) / coarse


def block_form(matrix):
    re, im = matrix.real, matrix.imag
    return np.stack([np.stack([re, -im], 1), np.stack([im, re], 1)], 0)


def halves(matrix):
    high = matrix.astype(ml_dtypes.bfloat16)
    low = (matrix - high.astype(np.float64)).astype(ml_dtypes.bfloat16)
    return high, low


def left_table(matrix):
    high, low = halves(matrix)
    return jnp.asarray(np.concatenate([high, high, low], axis=-1))


def right_table(matrix):
    high, low = halves(matrix)
    return jnp.asarray(np.concatenate([high, high, low], axis=-2))


def split(x):
    high = x.astype(BF16)
    return high, (x - high.astype(F32)).astype(BF16)


def product_left(m, x, dims=NN):
    high, low = split(x)
    axis = dims[0][1][0]
    wide = jnp.concatenate([high, low, high], axis=axis)
    return lax.dot_general(m, wide, dimension_numbers=dims, preferred_element_type=F32)


def product_right(x, m):
    high, low = split(x)
    wide = jnp.concatenate([high, low, high], axis=1)
    return lax.dot_general(wide, m, dimension_numbers=NN, preferred_element_type=F32)


def times_i(x):
    half = x.shape[1] // 2
    return jnp.concatenate([-x[:, half:], x[:, :half]], axis=1)


def flip(me, bit):
    return me + bit - 2 * bit * ((me // bit) % 2)


def flips(me, code):
    for bit in (1, 2):
        if code & bit:
            me = flip(me, bit)
    return me


def remote(src, dst, sends, recvs, where):
    return pltpu.make_async_remote_copy(
        src_ref=src, dst_ref=dst, send_sem=sends, recv_sem=recvs,
        device_id=where, device_id_type=MESH,
    )


def exchange_body(
    fields, sources, green, h_s1, h_top, h_f2, h_inv, h_first, h_mid, h_fc,
    ts_out, tc_out,
    xs, s1, yr, s2, zr, gb, s4, fin, fb, sb, sums, cr, xr, cz, cg, st,
    w_s1, w_top, w_f2, w_inv, w_first, w_mid, w_fc,
    load_sem, step_sem, out_sem, local_sem,
    y_s, y_r, z_s, z_r, g_s, g_r, core_s, core_r, x_s, x_r, zc_s, zc_r,
    cy_s, cy_r, cx_s, cx_r, cc_s, cc_r, zb_s, zb_r, yh_s, yh_r,
):
    t, y, z = lax.axis_index("tx"), lax.axis_index("py"), lax.axis_index("pz")
    oy = 1 - y
    z_peer = [flips(z, j) for j in (1, 2, 3)]
    to_z = [{"pz": p} for p in z_peer]
    to_y = {"py": oy}
    core, far = flip(t, 1), flip(t, 2)
    to_core, to_x = {"tx": core}, {"tx": far}
    x_chunks = xs.shape[0]
    k_own = gb.shape[1]
    part = sums.shape[2]
    f_chunks = fin.shape[0]
    rows_h = part // PARTS
    lanes = s1.shape[5]
    coarse = green.shape[3]
    f1 = st.shape[1]

    loads = [
        pltpu.make_async_copy(sources.at[0, :, :, pl.ds(c * ROWS, ROWS), :], xs.at[c], load_sem.at[c])
        for c in range(x_chunks)
    ]
    tables = [
        pltpu.make_async_copy(src, dst, load_sem.at[x_chunks + i])
        for i, (src, dst) in enumerate(
            [
                (h_s1, w_s1), (h_top.at[y], w_top), (h_f2, w_f2), (h_inv, w_inv),
                (h_mid.at[z], w_mid), (h_first.at[y], w_first), (h_fc.at[y], w_fc),
                (green.at[:, pl.ds(y * k_own, k_own)], gb.at[:, :, y]),
            ]
        )
    ]
    order = (1, 3, 0, 2)
    per_block = part // ROWS

    def step_copies(i):
        row = flips(t, order[i // per_block]) * part + (i % per_block) * ROWS
        at = pl.ds(row, ROWS)
        slot = i % 2
        return (
            pltpu.make_async_copy(fields.at[:, :, at], fb.at[slot], step_sem.at[0, slot]),
            pltpu.make_async_copy(sources.at[:, :, at], sb.at[slot], step_sem.at[1, slot]),
        )

    tables[0].start()
    for c in loads:
        c.start()
    tables[1].start()
    for i in range(2):
        for c in step_copies(i):
            c.start()
    for c in tables[2:]:
        c.start()

    barrier = pltpu.get_barrier_semaphore()
    peers = to_z + [to_y, to_core, to_x]
    for where in peers:
        pl.semaphore_signal(barrier, inc=1, device_id=where, device_id_type=MESH)

    tables[0].wait()
    for c in loads:
        c.wait()

    def depth(c, _):
        for s in range(ROWS):
            re, im = xs[c, 0, :, s, :], xs[c, 1, :, s, :]
            both = jnp.concatenate(
                [jnp.concatenate([re, -im], axis=1), jnp.concatenate([im, re], axis=1)], axis=0
            )
            out = product_left(w_s1[...], both, NT)
            s1[:, :, :, c, s, :] = out.reshape(s1.shape[0], s1.shape[1], s1.shape[2], lanes)
        return 0

    lax.fori_loop(0, x_chunks, depth, 0)
    pl.semaphore_wait(barrier, len(peers))

    y_copies = [remote(s1.at[oy, g], yr.at[g], y_s.at[g], y_r.at[g], to_y) for g in range(GROUPS)]
    for c in y_copies:
        c.start()

    core_copies = [
        remote(sums.at[j], cr.at[n], core_s.at[n], core_r.at[n], to_core)
        for n, j in enumerate((1, 3))
    ]
    steps = len(order) * per_block

    def sum_step(i):
        slot, block, base = i % 2, order[i // per_block], (i % per_block) * ROWS
        for c in step_copies(i):
            c.wait()

        def row(r, _):
            total = None
            for k in range(fb.shape[1]):
                fr, fi = fb[slot, k, 0, r], fb[slot, k, 1, r]
                sr, si = sb[slot, k, 0, r], sb[slot, k, 1, r]
                term = (sr * fr + si * fi, si * fr - sr * fi, fr * fr + fi * fi)
                total = term if total is None else tuple(a + b for a, b in zip(total, term))
            for n in range(3):
                sums[block, n, base + r] = total[n]
            return 0

        lax.fori_loop(0, ROWS, row, 0)
        if i + 2 < steps:
            for c in step_copies(i + 2):
                c.start()

    def sum_block(b):
        for i in range(b * per_block, (b + 1) * per_block):
            sum_step(i)

    def z_copy(g, n):
        p = z_peer[n]
        return remote(s2.at[g, p], zr.at[g, :, z], z_s.at[g, n], z_r.at[g, n], to_z[n])

    def top(g):
        y_copies[g].wait_recv()
        rows = s1.shape[2] * s1.shape[3] * ROWS
        own = s1[y, g].reshape(rows, lanes)
        other = yr[g].reshape(rows, lanes)
        out = product_right(jnp.concatenate([own, other], axis=1), w_top[...])
        s2[g] = out.reshape(s2.shape[1:])
        for n in (2, 1, 0):
            z_copy(g, n).start()
        zr[g, :, z] = s2[g, z]

    sum_block(0)
    core_copies[0].start()
    sum_block(1)
    core_copies[1].start()
    tables[1].wait()
    top(0)
    green_copy = remote(
        green.at[:, pl.ds(oy * k_own, k_own)], gb.at[:, :, y], g_s.at[0], g_r.at[0], to_y
    )
    sum_block(2)
    sum_block(3)
    top(1)
    green_copy.start()
    for n, j in enumerate((0, 2)):
        core_copies[n].wait_recv()

        def add(r, _, n=n, j=j):
            for k in range(3):
                sums[j, k, r] = sums[j, k, r] + cr[n, k, r]
            return 0

        lax.fori_loop(0, part, add, 0)
    x_copies = []
    for h in range(PARTS):
        at = pl.ds(h * rows_h, rows_h)
        x_copies.append(remote(sums.at[2, :, at], xr.at[:, at], x_s.at[h], x_r.at[h], to_x))
    for c in x_copies:
        c.start()
    top(2)
    top(3)

    def arrive(g):
        for n in range(3):
            z_copy(g, n).wait_recv()

    def middle(g):
        def one(i, _):
            x = zr[g, i].reshape(coarse, 2 * coarse)
            v = product_left(w_f2[...], jnp.concatenate([x, times_i(x)], axis=0))
            k = g * (k_own // GROUPS) + i
            gr, gi = gb[0, k].reshape(coarse, coarse), gb[1, k].reshape(coarse, coarse)
            vr, vi = v[:, :coarse], v[:, coarse:]
            w = jnp.concatenate([vr * gr - vi * gi, vr * gi + vi * gr], axis=1)
            u = product_left(w_inv[...], jnp.concatenate([w, times_i(w)], axis=0))
            s4[:, :, k] = u.reshape(s4.shape[0], s4.shape[1], ROWS, 2 * coarse)
            return 0

        lax.fori_loop(0, k_own // GROUPS, one, 0)

    def z_slice(h, src):
        return cz.at[:, pl.ds(h * rows_h, rows_h), src]

    def zc_copy(h, kind):
        src = z_peer[1] if kind == 2 else z
        where = to_z[1] if kind == 0 else to_z[0]
        return remote(z_slice(h, src), z_slice(h, src), zc_s.at[kind, h], zc_r.at[kind, h], where)

    def ratio(h):
        x_copies[h].wait_recv()
        for r in range(h * rows_h, (h + 1) * rows_h):
            nr = sums[0, 0, r] + xr[0, r]
            ni = sums[0, 1, r] + xr[1, r]
            d = sums[0, 2, r] + xr[2, r]
            cz[0, r, z] = nr / d
            cz[1, r, z] = ni / d
        zc_copy(h, 0).start()
        zc_copy(h, 1).start()

    def piece(a, b, h):
        return cg.at[a, b, :, :, pl.ds(h * rows_h, rows_h)]

    def pass_on(a, b, h, sends, recvs, where):
        return remote(piece(a, b, h), piece(a, b, h), sends, recvs, where)

    def cy_copy(h):
        return pass_on(y, t, h, cy_s.at[h], cy_r.at[h], to_y)

    def cx_copy(n, h):
        return pass_on((y, oy)[n], t, h, cx_s.at[n, h], cx_r.at[n, h], to_x)

    def cc_copy(n, h):
        return pass_on((y, oy)[n % 2], (t, far)[n // 2], h, cc_s.at[n, h], cc_r.at[n, h], to_core)

    tables[4].wait()
    half = cg.shape[2] * ROWS

    def refine(h):
        zc_copy(h, 1).wait_recv()
        zc_copy(h, 2).wait_recv()
        for r in range(h * rows_h, (h + 1) * rows_h):
            x = jnp.concatenate([cz[0, r].reshape(coarse, coarse), cz[1, r].reshape(coarse, coarse)], axis=0)
            out = product_left(w_mid[...], x)
            for c in range(2):
                cg[y, t, :, c, r] = out[c * half : (c + 1) * half].reshape(cg.shape[2], ROWS, coarse)
        cy_copy(h).start()
        cx_copy(0, h).start()
        cc_copy(0, h).start()

    cut = k_own - k_own // GROUPS
    early = 2

    def zb_copy(j, h, n):
        ks = pl.ds(0, cut) if h == 0 else pl.ds(cut, k_own - cut)
        return remote(
            s4.at[z_peer[n], j, ks], fin.at[j, y, z, ks],
            zb_s.at[j, h, n], zb_r.at[j, h, n], to_z[n],
        )

    def send_z(j, h):
        for n in (2, 1, 0):
            zb_copy(j, h, n).start()

    for h in range(PARTS):
        ratio(h)
    for n in (2, 3, 7):
        tables[n].wait()
    green_copy.wait_recv()
    for g in (0, 1):
        arrive(g)
        middle(g)
    for h in range(PARTS):
        zc_copy(h, 0).wait_recv()
        zc_copy(h, 2).start()
    arrive(2)
    middle(2)
    for h in range(PARTS):
        refine(h)
    arrive(3)
    for j in range(early):
        send_z(j, 0)
    middle(3)
    own_copy = pltpu.make_async_copy(s4.at[z], fin.at[:, y, z], local_sem.at[0])
    own_copy.start()
    for j in range(early):
        send_z(j, 1)

    def send_rest(j, _):
        send_z(j, 0)
        send_z(j, 1)
        return 0

    lax.fori_loop(early, f_chunks, send_rest, 0)

    def yh_copy(j):
        return remote(fin.at[j, y], fin.at[j, y], yh_s.at[j], yh_r.at[j], to_y)

    def out_copy(target, j, slot):
        return pltpu.make_async_copy(
            st.at[slot], target.at[:, pl.ds(j * ROWS, ROWS), :], out_sem.at[slot]
        )

    def emit(out, slot, s):
        st[slot, :, s, pl.ds(0, coarse)] = out[:f1]
        st[slot, :, s, pl.ds(coarse, coarse)] = out[f1:]

    def first_spec(j, slot):
        for s in range(ROWS):
            x = fin[j, :, :, :, s, :].reshape(coarse, 2 * coarse)
            emit(product_left(w_first[...], x, NT), slot, s)
        out_copy(ts_out, j, slot).start()

    def first_contrast(j, slot):
        for s in range(ROWS):
            x = cg[:, :, j, :, :, s, :].reshape(2 * coarse, coarse)
            emit(product_left(w_fc[...], x), slot, s)
        out_copy(tc_out, j, slot).start()

    own_copy.wait()
    tables[5].wait()
    tables[6].wait()
    lag = 2

    def contrast_step(j, _):
        @pl.when(j > 0)
        def _():
            out_copy(tc_out, j - 1, 1).wait()

        first_contrast(j, 1)
        return 0

    def forward(j, _):
        for h in range(2):
            for n in range(3):
                zb_copy(j, h, n).wait_recv()
        yh_copy(j).start()

        @pl.when(j == 0)
        def _():
            for h in range(PARTS):
                cy_copy(h).wait_recv()
                cx_copy(1, h).start()
                cc_copy(1, h).start()

        @pl.when(j == 1)
        def _():
            for h in range(PARTS):
                cx_copy(0, h).wait_recv()
                cc_copy(2, h).start()

        @pl.when(j == 3)
        def _():
            for h in range(PARTS):
                cx_copy(1, h).wait_recv()
                cc_copy(3, h).start()

        @pl.when(j >= lag)
        def _():
            yh_copy(j - lag).wait_recv()

            @pl.when(j > lag)
            def _():
                out_copy(ts_out, j - lag - 1, 0).wait()

            first_spec(j - lag, 0)

        @pl.when(j == f_chunks // 2)
        def _():
            for h in range(PARTS):
                for n in range(4):
                    cc_copy(n, h).wait_recv()

        @pl.when(j >= f_chunks // 2)
        def _():
            at = 2 * (j - f_chunks // 2)
            lax.fori_loop(at, at + 2, contrast_step, 0)

        return 0

    lax.fori_loop(0, f_chunks, forward, 0)

    def tail(j, _):
        yh_copy(j).wait_recv()
        out_copy(ts_out, j - 1, 0).wait()
        first_spec(j, 0)
        return 0

    lax.fori_loop(f_chunks - lag, f_chunks, tail, 0)

    for c in y_copies + core_copies + x_copies + [green_copy]:
        c.wait_send()
    for g in range(GROUPS):
        for n in range(3):
            z_copy(g, n).wait_send()
    for h in range(PARTS):
        for n in range(3):
            zc_copy(h, n).wait_send()
        cy_copy(h).wait_send()
        for n in range(2):
            cx_copy(n, h).wait_send()
        for n in range(4):
            cc_copy(n, h).wait_send()

    def drain(j, _):
        for h in range(2):
            for n in range(3):
                zb_copy(j, h, n).wait_send()
        yh_copy(j).wait_send()
        return 0

    lax.fori_loop(0, f_chunks, drain, 0)
    out_copy(tc_out, f_chunks - 1, 1).wait()
    out_copy(ts_out, f_chunks - 1, 0).wait()


def last_body(m3_ref, m3c_ref, ts_ref, tc_ref, c_ref, o_ref):
    f1, rows, wide = ts_ref.shape
    fine = m3_ref.shape[1] // 2
    step = max(1, 256 // rows)
    for b in range(0, f1, step):
        at = slice(b, b + step)
        d = product_right(ts_ref[at].reshape(step * rows, wide), m3_ref[...])
        c = product_right(tc_ref[at].reshape(step * rows, wide), m3c_ref[...])
        dr, di, cr, ci = d[:, :fine], d[:, fine:], c[:, :fine], c[:, fine:]
        shape = (step, rows, fine)
        c_ref[0, at] = cr.reshape(shape)
        c_ref[1, at] = ci.reshape(shape)
        o_ref[0, 0, at] = (cr * dr - ci * di).reshape(shape)
        o_ref[0, 1, at] = (cr * di + ci * dr).reshape(shape)


def fused_device(tx, py, pz, fields, sources, green):
    coarse = fields.shape[4]
    fine = 2 * coarse
    many = fields.shape[0]
    x1, x2 = fields.shape[2], fields.shape[3]
    f1, f2 = fine // py, fine // pz
    lanes = 2 * x1
    part = x1 // tx
    k3 = coarse // pz
    k_own = k3 // py
    k_group = k_own // GROUPS
    x_chunks, f_chunks = x2 // ROWS, f2 // ROWS

    fwd, inv = forward_matrix(coarse), inverse_matrix(coarse, fine)
    refined = inv @ fwd
    ri = lambda m: np.concatenate([m.real, m.imag], axis=1)
    grid = np.arange(coarse).reshape(pz, py, GROUPS, k_group)
    rows_s1 = grid.transpose(1, 2, 0, 3).reshape(-1)
    rows_k3 = grid.transpose(1, 0, 2, 3).reshape(-1)
    h_s1 = left_table(ri(fwd)[rows_s1])
    top = block_form(fwd).reshape(2 * coarse, 2, py, x1).transpose(2, 1, 3, 0)
    h_top = right_table(
        np.stack([top[[q, 1 - q]].reshape(2 * coarse, 2 * coarse) for q in range(py)])
    )
    h_f2 = left_table(ri(fwd))
    h_inv = left_table(ri(inv))
    first = block_form(inv).reshape(2, py, f1, 2 * coarse).transpose(1, 0, 2, 3)
    h_first = left_table(first.reshape(py, 2 * f1, 2 * coarse))
    mid = block_form(refined).reshape(2, pz, f2, 2 * coarse).transpose(1, 0, 2, 3)
    h_mid = left_table(mid.reshape(pz, 2 * f2, 2 * coarse))
    fc = block_form(refined).reshape(2, py, f1, 2, py, tx, part).transpose(1, 0, 2, 4, 5, 3, 6)
    h_fc = left_table(fc.reshape(py, 2 * f1, 2 * coarse))
    last = block_form(inv).transpose(2, 3, 0, 1)[:, rows_k3].reshape(2 * coarse, 2 * fine)
    last_c = block_form(refined).transpose(2, 3, 0, 1).reshape(2 * coarse, 2 * fine)
    m3, m3c = right_table(last), right_table(last_c)

    vm = lambda *dims: pltpu.VMEM(dims, F32)
    wm = lambda *dims: pltpu.VMEM(dims, BF16)
    dma = lambda *dims: pltpu.SemaphoreType.DMA(dims)
    pair = lambda *dims: [dma(*dims), dma(*dims)]
    wide = 2 * coarse
    scratch = [
        vm(x_chunks, 2, x1, ROWS, coarse),
        vm(py, GROUPS, pz * k_group, x_chunks, ROWS, lanes),
        vm(GROUPS, pz * k_group, x_chunks, ROWS, lanes),
        vm(GROUPS, pz, k_group, x2, wide),
        vm(GROUPS, k_group, pz, x2, wide),
        vm(2, k_own, py, coarse // py, coarse),
        vm(pz, f_chunks, k_own, ROWS, wide),
        vm(f_chunks, py, pz, k_own, ROWS, wide),
        vm(2, many, 2, ROWS, x2, coarse),
        vm(2, many, 2, ROWS, x2, coarse),
        vm(tx, 3, part, x2, coarse),
        vm(2, 3, part, x2, coarse),
        vm(3, part, x2, coarse),
        vm(2, part, pz, x2, coarse),
        vm(py, tx, f_chunks, 2, part, ROWS, coarse),
        vm(2, f1, ROWS, wide),
        wm(*h_s1.shape), wm(*h_top.shape[1:]), wm(*h_f2.shape), wm(*h_inv.shape),
        wm(*h_first.shape[1:]), wm(*h_mid.shape[1:]), wm(*h_fc.shape[1:]),
        dma(x_chunks + 8), dma(2, 2), dma(2), dma(1),
        *pair(GROUPS), *pair(GROUPS, 3), *pair(1), *pair(2), *pair(PARTS), *pair(3, PARTS),
        *pair(PARTS), *pair(2, PARTS), *pair(4, PARTS), *pair(f_chunks, 2, 3), *pair(f_chunks),
    ]
    middle_shape = jax.ShapeDtypeStruct((f1, f2, wide), F32)
    operands = (fields, sources, green, h_s1, h_top, h_f2, h_inv, h_first, h_mid, h_fc)
    anywhere = pl.BlockSpec(memory_space=pl.ANY)
    ts, tc = pl.pallas_call(
        exchange_body,
        in_specs=[anywhere] * len(operands),
        out_specs=[anywhere] * 2,
        out_shape=[middle_shape] * 2,
        scratch_shapes=scratch,
        name="exchange",
        compiler_params=pltpu.CompilerParams(
            collective_id=0, has_side_effects=True, vmem_limit_bytes=63 * 2**20
        ),
    )(*operands)

    blocked = pl.BlockSpec((f1, ROWS, wide), lambda i: (0, i, 0))
    whole = pl.BlockSpec(m3.shape, lambda i: (0, 0))
    return pl.pallas_call(
        last_body,
        grid=(f_chunks,),
        in_specs=[whole, whole, blocked, blocked],
        out_specs=[
            pl.BlockSpec((2, f1, ROWS, fine), lambda i: (0, 0, i, 0)),
            pl.BlockSpec((1, 2, f1, ROWS, fine), lambda i: (0, 0, 0, i, 0)),
        ],
        out_shape=[
            jax.ShapeDtypeStruct((2, f1, f2, fine), F32),
            jax.ShapeDtypeStruct((1, 2, f1, f2, fine), F32),
        ],
        name="last",
        compiler_params=pltpu.CompilerParams(vmem_limit_bytes=48 * 2**20),
    )(m3, m3c, ts, tc)


def fourier_matrix(out_index, in_index, period, exponent_sign, weight):
    phases = out_index[:, None] * in_index[None, :] % period
    angles = exponent_sign * 2.0 * math.pi / period * phases.astype(jnp.float32)
    cosine = weight * jnp.cos(angles)
    sine_part = weight * jnp.sin(angles)
    return jnp.stack([jnp.stack([cosine, -sine_part], 1), jnp.stack([sine_part, cosine], 1)], 0)


def local_step(values, matrix):
    return jnp.einsum("fcxyl,dkcl->fdyxk", values, matrix, precision=lax.Precision.HIGHEST)


def remote_step(values, matrix):
    return jnp.einsum("fclxy,dkcl->fdxyk", values, matrix, precision=lax.Precision.HIGHEST)


def turn(values, matrix, axis):
    return remote_step(lax.all_to_all(values, axis, split_axis=4, concat_axis=2, tiled=True), matrix)


def forward_pass(values, matrix):
    return turn(turn(local_step(values, matrix), matrix, "pz"), matrix, "py")


def inverse_pass(values, matrix):
    return turn(turn(local_step(values, matrix), matrix, "py"), matrix, "pz")


def complex_product(first_factor, second_factor):
    real_part = first_factor[0] * second_factor[0] - first_factor[1] * second_factor[1]
    imag_part = first_factor[0] * second_factor[1] + first_factor[1] * second_factor[0]
    return jnp.stack([real_part, imag_part])


def general_device(fields, sources, green):
    coarse = fields.shape[4]
    fine = 2 * coarse
    index = jnp.arange(coarse, dtype=jnp.int32)
    fine_index = jnp.arange(fine, dtype=jnp.int32)
    signed_coarse = jnp.where(index < coarse // 2, index, index - coarse)
    unit_coarse = jnp.ones((coarse, 1), F32)
    unit_fine = jnp.ones((fine, 1), F32)
    coarse_forward = fourier_matrix(index, index, coarse, -1.0, unit_coarse)
    padded_inverse = fourier_matrix(fine_index, signed_coarse, fine, 1.0, unit_fine / coarse)
    fr, fi, sr, si = fields[:, 0], fields[:, 1], sources[:, 0], sources[:, 1]
    numer_re = jnp.sum(sr * fr + si * fi, axis=0)
    numer_im = jnp.sum(si * fr - sr * fi, axis=0)
    denom = jnp.sum(fr * fr + fi * fi, axis=0)
    numer_re, numer_im, denom = lax.psum((numer_re, numer_im, denom), "tx")
    contrast = jnp.stack([numer_re / denom, numer_im / denom])[None]
    contrast_fine = inverse_pass(forward_pass(contrast, coarse_forward), padded_inverse)[0]
    spectrum = forward_pass(sources[0:1], coarse_forward)
    weighted = complex_product(spectrum[0], green)[None]
    domain_field = inverse_pass(weighted, padded_inverse)[0]
    return contrast_fine, complex_product(contrast_fine, domain_field)[None]


def solution(mesh):
    tx, py, pz = mesh.shape["tx"], mesh.shape["py"], mesh.shape["pz"]

    def on_device(fields, sources, green):
        x1, x2, coarse = fields.shape[2:]
        fused = (
            tx == 4 and py == 2 and pz == 4
            and coarse % 128 == 0 and (2 * x1) % 128 == 0 and x1 % (tx * ROWS) == 0
            and x2 % ROWS == 0 and (2 * coarse // pz) % (2 * ROWS) == 0 and 2 * coarse // pz >= 8 * ROWS
            and coarse % (pz * py * GROUPS) == 0 and x1 % (tx * PARTS) == 0
            and coarse * coarse * coarse <= 2**21
        )
        if fused:
            return fused_device(tx, py, pz, fields, sources, green)
        return general_device(fields, sources, green)

    placed = (
        P("tx", None, "py", "pz", None),
        P("tx", None, "py", "pz", None),
        P(None, "pz", "py", None),
    )
    return jax.shard_map(
        on_device,
        mesh=mesh,
        in_specs=placed,
        out_specs=(P(None, "py", "pz", None), P("tx", None, "py", "pz", None)),
        check_vma=False,
    )
```

```python
import functools
import math

import jax
import jax.numpy as jnp
import ml_dtypes
import numpy as np
from jax import lax
from jax.experimental import pallas as pl
from jax.experimental.pallas import tpu as pltpu
from jax.sharding import PartitionSpec as P

F32 = jnp.float32
BF16 = jnp.bfloat16
NN = (((1,), (0,)), ((), ()))
NT = (((1,), (1,)), ((), ()))
MESH = pl.DeviceIdType.MESH
ROWS = 8
GROUPS = 4
PARTS = 4


def signed(count):
    index = np.arange(count)
    return np.where(index < count // 2, index, index - count)


def forward_matrix(coarse):
    index = np.arange(coarse)
    return np.exp(-2j * np.pi * ((index[:, None] * index[None, :]) % coarse) / coarse)


def inverse_matrix(coarse, fine):
    phases = (np.arange(fine)[:, None] * signed(coarse)[None, :]) % fine
    return np.exp(2j * np.pi * phases / fine) / coarse


def block_form(matrix):
    re, im = matrix.real, matrix.imag
    return np.stack([np.stack([re, -im], 1), np.stack([im, re], 1)], 0)


def halves(matrix):
    high = matrix.astype(ml_dtypes.bfloat16)
    low = (matrix - high.astype(np.float64)).astype(ml_dtypes.bfloat16)
    return high, low


def left_table(matrix):
    high, low = halves(matrix)
    return jnp.asarray(np.concatenate([high, high, low], axis=-1))


def right_table(matrix):
    high, low = halves(matrix)
    return jnp.asarray(np.concatenate([high, high, low], axis=-2))


def split(x):
    high = x.astype(BF16)
    return high, (x - high.astype(F32)).astype(BF16)


def product_left(m, x, dims=NN):
    high, low = split(x)
    axis = dims[0][1][0]
    wide = jnp.concatenate([high, low, high], axis=axis)
    return lax.dot_general(m, wide, dimension_numbers=dims, preferred_element_type=F32)


def product_right(x, m):
    high, low = split(x)
    wide = jnp.concatenate([high, low, high], axis=1)
    return lax.dot_general(wide, m, dimension_numbers=NN, preferred_element_type=F32)


def times_i(x):
    half = x.shape[1] // 2
    return jnp.concatenate([-x[:, half:], x[:, :half]], axis=1)


def flip(me, bit):
    return me + bit - 2 * bit * ((me // bit) % 2)


def flips(me, code):
    for bit in (1, 2):
        if code & bit:
            me = flip(me, bit)
    return me


def remote(src, dst, sends, recvs, where):
    return pltpu.make_async_remote_copy(
        src_ref=src, dst_ref=dst, send_sem=sends, recv_sem=recvs,
        device_id=where, device_id_type=MESH,
    )


def exchange_body(
    fields, sources, green, h_s1, h_top, h_f2, h_inv, h_first, h_mid, h_fc,
    ts_out, tc_out,
    xs, s1, yr, s2, zr, gb, s4, fin, fb, sb, sums, cr, xr, cz, cg, st,
    w_s1, w_top, w_f2, w_inv, w_first, w_mid, w_fc,
    load_sem, step_sem, out_sem, local_sem,
    y_s, y_r, z_s, z_r, g_s, g_r, core_s, core_r, x_s, x_r, zc_s, zc_r,
    cy_s, cy_r, cx_s, cx_r, cc_s, cc_r, zb_s, zb_r, yh_s, yh_r,
):
    t, y, z = lax.axis_index("tx"), lax.axis_index("py"), lax.axis_index("pz")
    oy = 1 - y
    z_peer = [flips(z, j) for j in (1, 2, 3)]
    to_z = [{"pz": p} for p in z_peer]
    to_y = {"py": oy}
    core, far = flip(t, 1), flip(t, 2)
    to_core, to_x = {"tx": core}, {"tx": far}
    x_chunks = xs.shape[0]
    k_own = gb.shape[1]
    part = sums.shape[2]
    f_chunks = fin.shape[0]
    rows_h = part // PARTS
    lanes = s1.shape[5]
    coarse = green.shape[3]
    f1 = st.shape[1]

    loads = [
        pltpu.make_async_copy(sources.at[0, :, :, pl.ds(c * ROWS, ROWS), :], xs.at[c], load_sem.at[c])
        for c in range(x_chunks)
    ]
    tables = [
        pltpu.make_async_copy(src, dst, load_sem.at[x_chunks + i])
        for i, (src, dst) in enumerate(
            [
                (h_s1, w_s1), (h_top.at[y], w_top), (h_f2, w_f2), (h_inv, w_inv),
                (h_mid.at[z], w_mid), (h_first.at[y], w_first), (h_fc.at[y], w_fc),
                (green.at[:, pl.ds(y * k_own, k_own)], gb.at[:, :, y]),
            ]
        )
    ]
    order = (1, 3, 0, 2)
    per_block = part // ROWS

    def step_copies(i):
        row = flips(t, order[i // per_block]) * part + (i % per_block) * ROWS
        at = pl.ds(row, ROWS)
        slot = i % 2
        return (
            pltpu.make_async_copy(fields.at[:, :, at], fb.at[slot], step_sem.at[0, slot]),
            pltpu.make_async_copy(sources.at[:, :, at], sb.at[slot], step_sem.at[1, slot]),
        )

    tables[0].start()
    for c in loads:
        c.start()
    tables[1].start()
    for i in range(2):
        for c in step_copies(i):
            c.start()
    for c in tables[2:]:
        c.start()

    barrier = pltpu.get_barrier_semaphore()
    peers = to_z + [to_y, to_core, to_x]
    for where in peers:
        pl.semaphore_signal(barrier, inc=1, device_id=where, device_id_type=MESH)

    tables[0].wait()
    for c in loads:
        c.wait()

    def depth(c, _):
        for s in range(ROWS):
            re, im = xs[c, 0, :, s, :], xs[c, 1, :, s, :]
            both = jnp.concatenate(
                [jnp.concatenate([re, -im], axis=1), jnp.concatenate([im, re], axis=1)], axis=0
            )
            out = product_left(w_s1[...], both, NT)
            s1[:, :, :, c, s, :] = out.reshape(s1.shape[0], s1.shape[1], s1.shape[2], lanes)
        return 0

    lax.fori_loop(0, x_chunks, depth, 0)
    pl.semaphore_wait(barrier, len(peers))

    y_copies = [remote(s1.at[oy, g], yr.at[g], y_s.at[g], y_r.at[g], to_y) for g in range(GROUPS)]
    for c in y_copies:
        c.start()

    core_copies = [
        remote(sums.at[j], cr.at[n], core_s.at[n], core_r.at[n], to_core)
        for n, j in enumerate((1, 3))
    ]
    steps = len(order) * per_block

    def sum_step(i):
        slot, block, base = i % 2, order[i // per_block], (i % per_block) * ROWS
        for c in step_copies(i):
            c.wait()

        def row(r, _):
            total = None
            for k in range(fb.shape[1]):
                fr, fi = fb[slot, k, 0, r], fb[slot, k, 1, r]
                sr, si = sb[slot, k, 0, r], sb[slot, k, 1, r]
                term = (sr * fr + si * fi, si * fr - sr * fi, fr * fr + fi * fi)
                total = term if total is None else tuple(a + b for a, b in zip(total, term))
            for n in range(3):
                sums[block, n, base + r] = total[n]
            return 0

        lax.fori_loop(0, ROWS, row, 0)
        if i + 2 < steps:
            for c in step_copies(i + 2):
                c.start()

    def sum_block(b):
        for i in range(b * per_block, (b + 1) * per_block):
            sum_step(i)

    def z_copy(g, n):
        p = z_peer[n]
        return remote(s2.at[g, p], zr.at[g, :, z], z_s.at[g, n], z_r.at[g, n], to_z[n])

    def top(g):
        y_copies[g].wait_recv()
        rows = s1.shape[2] * s1.shape[3] * ROWS
        own = s1[y, g].reshape(rows, lanes)
        other = yr[g].reshape(rows, lanes)
        out = product_right(jnp.concatenate([own, other], axis=1), w_top[...])
        s2[g] = out.reshape(s2.shape[1:])
        zr[g, :, z] = s2[g, z]

    def send_top(g):
        for n in (2, 1, 0):
            z_copy(g, n).start()

    sum_block(0)
    core_copies[0].start()
    sum_block(1)
    core_copies[1].start()
    tables[1].wait()
    top(0)
    send_top(0)
    green_copy = remote(
        green.at[:, pl.ds(oy * k_own, k_own)], gb.at[:, :, y], g_s.at[0], g_r.at[0], to_y
    )
    sum_block(2)
    sum_block(3)
    top(1)
    send_top(1)
    green_copy.start()
    for n, j in enumerate((0, 2)):
        core_copies[n].wait_recv()

        def add(r, _, n=n, j=j):
            for k in range(3):
                sums[j, k, r] = sums[j, k, r] + cr[n, k, r]
            return 0

        lax.fori_loop(0, part, add, 0)
    x_copies = []
    for h in range(PARTS):
        at = pl.ds(h * rows_h, rows_h)
        x_copies.append(remote(sums.at[2, :, at], xr.at[:, at], x_s.at[h], x_r.at[h], to_x))
    for c in x_copies:
        c.start()
    top(2)
    top(3)

    def arrive(g):
        for n in range(3):
            z_copy(g, n).wait_recv()

    def middle(g):
        def one(i, _):
            x = zr[g, i].reshape(coarse, 2 * coarse)
            v = product_left(w_f2[...], jnp.concatenate([x, times_i(x)], axis=0))
            k = g * (k_own // GROUPS) + i
            gr, gi = gb[0, k].reshape(coarse, coarse), gb[1, k].reshape(coarse, coarse)
            vr, vi = v[:, :coarse], v[:, coarse:]
            w = jnp.concatenate([vr * gr - vi * gi, vr * gi + vi * gr], axis=1)
            u = product_left(w_inv[...], jnp.concatenate([w, times_i(w)], axis=0))
            s4[:, :, k] = u.reshape(s4.shape[0], s4.shape[1], ROWS, 2 * coarse)
            return 0

        lax.fori_loop(0, k_own // GROUPS, one, 0)

    def z_slice(h, src):
        return cz.at[:, pl.ds(h * rows_h, rows_h), src]

    def zc_copy(h, kind):
        src = z_peer[1] if kind == 2 else z
        where = to_z[1] if kind == 0 else to_z[0]
        return remote(z_slice(h, src), z_slice(h, src), zc_s.at[kind, h], zc_r.at[kind, h], where)

    def ratio(h):
        x_copies[h].wait_recv()
        for r in range(h * rows_h, (h + 1) * rows_h):
            nr = sums[0, 0, r] + xr[0, r]
            ni = sums[0, 1, r] + xr[1, r]
            d = sums[0, 2, r] + xr[2, r]
            cz[0, r, z] = nr / d
            cz[1, r, z] = ni / d
        zc_copy(h, 0).start()
        zc_copy(h, 1).start()

    def piece(a, b, h):
        return cg.at[a, b, :, :, pl.ds(h * rows_h, rows_h)]

    def pass_on(a, b, h, sends, recvs, where):
        return remote(piece(a, b, h), piece(a, b, h), sends, recvs, where)

    def cy_copy(h):
        return pass_on(y, t, h, cy_s.at[h], cy_r.at[h], to_y)

    def cx_copy(n, h):
        return pass_on((y, oy)[n], t, h, cx_s.at[n, h], cx_r.at[n, h], to_x)

    def cc_copy(n, h):
        return pass_on((y, oy)[n % 2], (t, far)[n // 2], h, cc_s.at[n, h], cc_r.at[n, h], to_core)

    tables[4].wait()
    half = cg.shape[2] * ROWS

    def refine(h):
        zc_copy(h, 1).wait_recv()
        zc_copy(h, 2).wait_recv()
        for r in range(h * rows_h, (h + 1) * rows_h):
            x = jnp.concatenate([cz[0, r].reshape(coarse, coarse), cz[1, r].reshape(coarse, coarse)], axis=0)
            out = product_left(w_mid[...], x)
            for c in range(2):
                cg[y, t, :, c, r] = out[c * half : (c + 1) * half].reshape(cg.shape[2], ROWS, coarse)
        cy_copy(h).start()
        cx_copy(0, h).start()
        cc_copy(0, h).start()

    cut = k_own - k_own // GROUPS
    early = 2

    def zb_copy(j, h, n):
        ks = pl.ds(0, cut) if h == 0 else pl.ds(cut, k_own - cut)
        return remote(
            s4.at[z_peer[n], j, ks], fin.at[j, y, z, ks],
            zb_s.at[j, h, n], zb_r.at[j, h, n], to_z[n],
        )

    def send_z(j, h):
        for n in (2, 1, 0):
            zb_copy(j, h, n).start()

    for h in range(PARTS):
        ratio(h)
    send_top(2)
    for n in (2, 3, 7):
        tables[n].wait()
    green_copy.wait_recv()
    for g in (0, 1):
        arrive(g)
        middle(g)
    for h in range(PARTS):
        zc_copy(h, 0).wait_recv()
        zc_copy(h, 2).start()
    send_top(3)
    arrive(2)
    middle(2)
    for j in range(early):
        send_z(j, 0)
    for h in range(PARTS):
        refine(h)
    arrive(3)
    middle(3)
    own_copy = pltpu.make_async_copy(s4.at[z], fin.at[:, y, z], local_sem.at[0])
    own_copy.start()
    for j in range(early):
        send_z(j, 1)

    def send_rest(j, _):
        send_z(j, 0)
        send_z(j, 1)
        return 0

    lax.fori_loop(early, f_chunks, send_rest, 0)

    def yh_copy(j):
        return remote(fin.at[j, y], fin.at[j, y], yh_s.at[j], yh_r.at[j], to_y)

    def out_copy(target, j, slot):
        return pltpu.make_async_copy(
            st.at[slot], target.at[:, pl.ds(j * ROWS, ROWS), :], out_sem.at[slot]
        )

    def emit(out, slot, s):
        st[slot, :, s, pl.ds(0, coarse)] = out[:f1]
        st[slot, :, s, pl.ds(coarse, coarse)] = out[f1:]

    def first_spec(j, slot):
        for s in range(ROWS):
            x = fin[j, :, :, :, s, :].reshape(coarse, 2 * coarse)
            emit(product_left(w_first[...], x, NT), slot, s)
        out_copy(ts_out, j, slot).start()

    def first_contrast(j, slot):
        for s in range(ROWS):
            x = cg[:, :, j, :, :, s, :].reshape(2 * coarse, coarse)
            emit(product_left(w_fc[...], x), slot, s)
        out_copy(tc_out, j, slot).start()

    own_copy.wait()
    tables[5].wait()
    tables[6].wait()
    lag = 2

    def contrast_step(j, _):
        @pl.when(j > 0)
        def _():
            out_copy(tc_out, j - 1, 1).wait()

        first_contrast(j, 1)
        return 0

    def forward(j, _):
        for h in range(2):
            for n in range(3):
                zb_copy(j, h, n).wait_recv()
        yh_copy(j).start()

        @pl.when(j == 0)
        def _():
            for h in range(PARTS):
                cy_copy(h).wait_recv()
                cx_copy(1, h).start()
                cc_copy(1, h).start()

        @pl.when(j == 1)
        def _():
            for h in range(PARTS):
                cx_copy(0, h).wait_recv()
                cc_copy(2, h).start()

        @pl.when(j == 3)
        def _():
            for h in range(PARTS):
                cx_copy(1, h).wait_recv()
                cc_copy(3, h).start()

        @pl.when(j >= lag)
        def _():
            yh_copy(j - lag).wait_recv()

            @pl.when(j > lag)
            def _():
                out_copy(ts_out, j - lag - 1, 0).wait()

            first_spec(j - lag, 0)

        @pl.when(j == f_chunks // 2)
        def _():
            for h in range(PARTS):
                for n in range(4):
                    cc_copy(n, h).wait_recv()

        @pl.when(j >= f_chunks // 2)
        def _():
            at = 2 * (j - f_chunks // 2)
            lax.fori_loop(at, at + 2, contrast_step, 0)

        return 0

    lax.fori_loop(0, f_chunks, forward, 0)

    def tail(j, _):
        yh_copy(j).wait_recv()
        out_copy(ts_out, j - 1, 0).wait()
        first_spec(j, 0)
        return 0

    lax.fori_loop(f_chunks - lag, f_chunks, tail, 0)

    for c in y_copies + core_copies + x_copies + [green_copy]:
        c.wait_send()
    for g in range(GROUPS):
        for n in range(3):
            z_copy(g, n).wait_send()
    for h in range(PARTS):
        for n in range(3):
            zc_copy(h, n).wait_send()
        cy_copy(h).wait_send()
        for n in range(2):
            cx_copy(n, h).wait_send()
        for n in range(4):
            cc_copy(n, h).wait_send()

    def drain(j, _):
        for h in range(2):
            for n in range(3):
                zb_copy(j, h, n).wait_send()
        yh_copy(j).wait_send()
        return 0

    lax.fori_loop(0, f_chunks, drain, 0)
    out_copy(tc_out, f_chunks - 1, 1).wait()
    out_copy(ts_out, f_chunks - 1, 0).wait()


def last_body(m3_ref, m3c_ref, ts_ref, tc_ref, c_ref, o_ref):
    f1, rows, wide = ts_ref.shape
    fine = m3_ref.shape[1] // 2
    step = max(1, 256 // rows)
    for b in range(0, f1, step):
        at = slice(b, b + step)
        d = product_right(ts_ref[at].reshape(step * rows, wide), m3_ref[...])
        c = product_right(tc_ref[at].reshape(step * rows, wide), m3c_ref[...])
        dr, di, cr, ci = d[:, :fine], d[:, fine:], c[:, :fine], c[:, fine:]
        shape = (step, rows, fine)
        c_ref[0, at] = cr.reshape(shape)
        c_ref[1, at] = ci.reshape(shape)
        o_ref[0, 0, at] = (cr * dr - ci * di).reshape(shape)
        o_ref[0, 1, at] = (cr * di + ci * dr).reshape(shape)


def fused_device(tx, py, pz, fields, sources, green):
    coarse = fields.shape[4]
    fine = 2 * coarse
    many = fields.shape[0]
    x1, x2 = fields.shape[2], fields.shape[3]
    f1, f2 = fine // py, fine // pz
    lanes = 2 * x1
    part = x1 // tx
    k3 = coarse // pz
    k_own = k3 // py
    k_group = k_own // GROUPS
    x_chunks, f_chunks = x2 // ROWS, f2 // ROWS

    fwd, inv = forward_matrix(coarse), inverse_matrix(coarse, fine)
    refined = inv @ fwd
    ri = lambda m: np.concatenate([m.real, m.imag], axis=1)
    grid = np.arange(coarse).reshape(pz, py, GROUPS, k_group)
    rows_s1 = grid.transpose(1, 2, 0, 3).reshape(-1)
    rows_k3 = grid.transpose(1, 0, 2, 3).reshape(-1)
    h_s1 = left_table(ri(fwd)[rows_s1])
    top = block_form(fwd).reshape(2 * coarse, 2, py, x1).transpose(2, 1, 3, 0)
    h_top = right_table(
        np.stack([top[[q, 1 - q]].reshape(2 * coarse, 2 * coarse) for q in range(py)])
    )
    h_f2 = left_table(ri(fwd))
    h_inv = left_table(ri(inv))
    first = block_form(inv).reshape(2, py, f1, 2 * coarse).transpose(1, 0, 2, 3)
    h_first = left_table(first.reshape(py, 2 * f1, 2 * coarse))
    mid = block_form(refined).reshape(2, pz, f2, 2 * coarse).transpose(1, 0, 2, 3)
    h_mid = left_table(mid.reshape(pz, 2 * f2, 2 * coarse))
    fc = block_form(refined).reshape(2, py, f1, 2, py, tx, part).transpose(1, 0, 2, 4, 5, 3, 6)
    h_fc = left_table(fc.reshape(py, 2 * f1, 2 * coarse))
    last = block_form(inv).transpose(2, 3, 0, 1)[:, rows_k3].reshape(2 * coarse, 2 * fine)
    last_c = block_form(refined).transpose(2, 3, 0, 1).reshape(2 * coarse, 2 * fine)
    m3, m3c = right_table(last), right_table(last_c)

    vm = lambda *dims: pltpu.VMEM(dims, F32)
    wm = lambda *dims: pltpu.VMEM(dims, BF16)
    dma = lambda *dims: pltpu.SemaphoreType.DMA(dims)
    pair = lambda *dims: [dma(*dims), dma(*dims)]
    wide = 2 * coarse
    scratch = [
        vm(x_chunks, 2, x1, ROWS, coarse),
        vm(py, GROUPS, pz * k_group, x_chunks, ROWS, lanes),
        vm(GROUPS, pz * k_group, x_chunks, ROWS, lanes),
        vm(GROUPS, pz, k_group, x2, wide),
        vm(GROUPS, k_group, pz, x2, wide),
        vm(2, k_own, py, coarse // py, coarse),
        vm(pz, f_chunks, k_own, ROWS, wide),
        vm(f_chunks, py, pz, k_own, ROWS, wide),
        vm(2, many, 2, ROWS, x2, coarse),
        vm(2, many, 2, ROWS, x2, coarse),
        vm(tx, 3, part, x2, coarse),
        vm(2, 3, part, x2, coarse),
        vm(3, part, x2, coarse),
        vm(2, part, pz, x2, coarse),
        vm(py, tx, f_chunks, 2, part, ROWS, coarse),
        vm(2, f1, ROWS, wide),
        wm(*h_s1.shape), wm(*h_top.shape[1:]), wm(*h_f2.shape), wm(*h_inv.shape),
        wm(*h_first.shape[1:]), wm(*h_mid.shape[1:]), wm(*h_fc.shape[1:]),
        dma(x_chunks + 8), dma(2, 2), dma(2), dma(1),
        *pair(GROUPS), *pair(GROUPS, 3), *pair(1), *pair(2), *pair(PARTS), *pair(3, PARTS),
        *pair(PARTS), *pair(2, PARTS), *pair(4, PARTS), *pair(f_chunks, 2, 3), *pair(f_chunks),
    ]
    middle_shape = jax.ShapeDtypeStruct((f1, f2, wide), F32)
    operands = (fields, sources, green, h_s1, h_top, h_f2, h_inv, h_first, h_mid, h_fc)
    anywhere = pl.BlockSpec(memory_space=pl.ANY)
    ts, tc = pl.pallas_call(
        exchange_body,
        in_specs=[anywhere] * len(operands),
        out_specs=[anywhere] * 2,
        out_shape=[middle_shape] * 2,
        scratch_shapes=scratch,
        name="exchange",
        compiler_params=pltpu.CompilerParams(
            collective_id=0, has_side_effects=True, vmem_limit_bytes=63 * 2**20
        ),
    )(*operands)

    blocked = pl.BlockSpec((f1, ROWS, wide), lambda i: (0, i, 0))
    whole = pl.BlockSpec(m3.shape, lambda i: (0, 0))
    return pl.pallas_call(
        last_body,
        grid=(f_chunks,),
        in_specs=[whole, whole, blocked, blocked],
        out_specs=[
            pl.BlockSpec((2, f1, ROWS, fine), lambda i: (0, 0, i, 0)),
            pl.BlockSpec((1, 2, f1, ROWS, fine), lambda i: (0, 0, 0, i, 0)),
        ],
        out_shape=[
            jax.ShapeDtypeStruct((2, f1, f2, fine), F32),
            jax.ShapeDtypeStruct((1, 2, f1, f2, fine), F32),
        ],
        name="last",
        compiler_params=pltpu.CompilerParams(vmem_limit_bytes=48 * 2**20),
    )(m3, m3c, ts, tc)


def fourier_matrix(out_index, in_index, period, exponent_sign, weight):
    phases = out_index[:, None] * in_index[None, :] % period
    angles = exponent_sign * 2.0 * math.pi / period * phases.astype(jnp.float32)
    cosine = weight * jnp.cos(angles)
    sine_part = weight * jnp.sin(angles)
    return jnp.stack([jnp.stack([cosine, -sine_part], 1), jnp.stack([sine_part, cosine], 1)], 0)


def local_step(values, matrix):
    return jnp.einsum("fcxyl,dkcl->fdyxk", values, matrix, precision=lax.Precision.HIGHEST)


def remote_step(values, matrix):
    return jnp.einsum("fclxy,dkcl->fdxyk", values, matrix, precision=lax.Precision.HIGHEST)


def turn(values, matrix, axis):
    return remote_step(lax.all_to_all(values, axis, split_axis=4, concat_axis=2, tiled=True), matrix)


def forward_pass(values, matrix):
    return turn(turn(local_step(values, matrix), matrix, "pz"), matrix, "py")


def inverse_pass(values, matrix):
    return turn(turn(local_step(values, matrix), matrix, "py"), matrix, "pz")


def complex_product(first_factor, second_factor):
    real_part = first_factor[0] * second_factor[0] - first_factor[1] * second_factor[1]
    imag_part = first_factor[0] * second_factor[1] + first_factor[1] * second_factor[0]
    return jnp.stack([real_part, imag_part])


def general_device(fields, sources, green):
    coarse = fields.shape[4]
    fine = 2 * coarse
    index = jnp.arange(coarse, dtype=jnp.int32)
    fine_index = jnp.arange(fine, dtype=jnp.int32)
    signed_coarse = jnp.where(index < coarse // 2, index, index - coarse)
    unit_coarse = jnp.ones((coarse, 1), F32)
    unit_fine = jnp.ones((fine, 1), F32)
    coarse_forward = fourier_matrix(index, index, coarse, -1.0, unit_coarse)
    padded_inverse = fourier_matrix(fine_index, signed_coarse, fine, 1.0, unit_fine / coarse)
    fr, fi, sr, si = fields[:, 0], fields[:, 1], sources[:, 0], sources[:, 1]
    numer_re = jnp.sum(sr * fr + si * fi, axis=0)
    numer_im = jnp.sum(si * fr - sr * fi, axis=0)
    denom = jnp.sum(fr * fr + fi * fi, axis=0)
    numer_re, numer_im, denom = lax.psum((numer_re, numer_im, denom), "tx")
    contrast = jnp.stack([numer_re / denom, numer_im / denom])[None]
    contrast_fine = inverse_pass(forward_pass(contrast, coarse_forward), padded_inverse)[0]
    spectrum = forward_pass(sources[0:1], coarse_forward)
    weighted = complex_product(spectrum[0], green)[None]
    domain_field = inverse_pass(weighted, padded_inverse)[0]
    return contrast_fine, complex_product(contrast_fine, domain_field)[None]


def solution(mesh):
    tx, py, pz = mesh.shape["tx"], mesh.shape["py"], mesh.shape["pz"]

    def on_device(fields, sources, green):
        x1, x2, coarse = fields.shape[2:]
        fused = (
            tx == 4 and py == 2 and pz == 4
            and coarse % 128 == 0 and (2 * x1) % 128 == 0 and x1 % (tx * ROWS) == 0
            and x2 % ROWS == 0 and (2 * coarse // pz) % (2 * ROWS) == 0 and 2 * coarse // pz >= 8 * ROWS
            and coarse % (pz * py * GROUPS) == 0 and x1 % (tx * PARTS) == 0
            and coarse * coarse * coarse <= 2**21
        )
        if fused:
            return fused_device(tx, py, pz, fields, sources, green)
        return general_device(fields, sources, green)

    placed = (
        P("tx", None, "py", "pz", None),
        P("tx", None, "py", "pz", None),
        P(None, "pz", "py", None),
    )
    return jax.shard_map(
        on_device,
        mesh=mesh,
        in_specs=placed,
        out_specs=(P(None, "py", "pz", None), P("tx", None, "py", "pz", None)),
        check_vma=False,
    )
```
